512 devices in a mesh: group: 16 (over y, x), dev: 32 (over z, core).
Axes of the slice: x: 4, y: 4, z: 16, core: 2. Of those that a mesh axis runs over, the one named last changes fastest.
Arguments:
- anchors: bfloat16 [32768, 256], P('dev'), may hold values from -6 to 6
- coefs: bfloat16 [1024, 64, 1024], P(('group', 'dev')), may hold values from -0.1875 to 0.1875
- block_cols: int32 [1024, 16], P(('group', 'dev')), may hold values from 0 to 511, as said below
- block_counts: int32 [1024], P(('group', 'dev')), may hold values from 8 to 16, as said below
- sample_rows: int32 [262144, 32], P(('group', 'dev')), may hold values from 0 to 127
- labels: int32 [262144], P(('group', 'dev')), may hold values 0 or 1
- pair_weights: float32 [32, 32], replicated, may hold values from -0.06 to 0.06
Outputs:
- update: float32 [32768, 256], P('dev')
- scores: float32 [262144], P(('group', 'dev'))
The draws below stay inside these ranges and needn't reach their ends.
Inputs may be any that keep to these rules, and one draw needn't show every extreme that they name: `block_cols`: ids of all slots, padded ones too. Over the 2 row blocks of one device, at most 2 slots name blocks 16 * o to 16 * (o + 1) - 1 for any o; in every group some o gets exactly 2 live slots from each device of the group. `block_counts`: on each device, the leading row blocks that together hold 2 live slots are full with 16 live slots each; every other row block holds at least 8.
All inputs are finite; a program needn't handle non-finite values. No bound on the sum of `labels` on one device may be relied on, other than what follows from the above.
Results may differ from the reference program's by a relative error of at most 0.015.
Values may be sent and summed in bfloat16 or wider, within the bound.
A program may use at most 64 MiB of HBM per device.

```python
import jax
import jax.numpy as jnp
from jax import lax

W = 256
F = 32
BLK = 64
SLOTS = 16
RB_DEV = 2
ANC_BLK_DEV = 16
SMP_DEV = 512
ROWS_DEV = 128
NRB = 1024
CAP = 2
BLOCKS = 512
ANCHORS = 32768
BATCH = 262144


def draw_block_counts(key, part):
    devices = NRB // RB_DEV
    full = (CAP + SLOTS - 1) // SLOTS
    half = SLOTS // 2
    first_key, second_key = jax.random.split(key)
    level = jax.random.randint(first_key, (devices, 1), 1, SLOTS - half + 2)
    raw = jax.random.randint(second_key, (devices, RB_DEV), 0, 1 << 20)
    counts = half + raw % level
    counts = jnp.where(jnp.arange(RB_DEV)[None, :] < full, SLOTS, counts)
    return counts.reshape(NRB).astype(jnp.int32)


def draw_block_cols(key, part):
    devices = NRB // RB_DEV
    holders = BLOCKS // ANC_BLK_DEV
    groups = devices // holders
    span = RB_DEV * SLOTS
    rest = span - CAP
    hot_key, perm_key, local_key = jax.random.split(key, 3)
    hot = jax.random.randint(hot_key, (groups,), 0, holders)
    hot_dev = jnp.repeat(hot, holders)
    pool = jnp.arange((holders - 1) * CAP) // CAP
    keys = jax.random.split(perm_key, devices)
    perms = jax.vmap(lambda single: jax.random.permutation(single, (holders - 1) * CAP))(keys)[:, :rest]
    others = pool[perms]
    others = others + (others >= hot_dev[:, None]).astype(jnp.int32)
    holder = jnp.concatenate([jnp.broadcast_to(hot_dev[:, None], (devices, CAP)), others], axis=1)
    local = jax.random.randint(local_key, (devices, span), 0, ANC_BLK_DEV)
    return (holder * ANC_BLK_DEV + local).reshape(NRB, SLOTS).astype(jnp.int32)


def set_ends(values, stream_key, smallest, high):
    shape = values.shape
    index_at = [jax.random.randint(jax.random.fold_in(stream_key, axis), (), 0, shape[axis]) for axis in range(len(shape))]
    values = values.at[tuple(index_at)].set(smallest)
    longest = shape.index(max(shape))
    index_at[longest] = (index_at[longest] + 1) % shape[longest]
    return values.at[tuple(index_at)].set(high)


def steps_of(own_key, extent, pieces, smallest, largest):
    def one(axis_at, blocks):
        heights = jax.random.uniform(jax.random.fold_in(jax.random.fold_in(own_key, 6), axis_at), (blocks,), jnp.float32, smallest / len(pieces), largest / len(pieces))
        return jnp.repeat(jnp.exp(heights), extent[axis_at] // blocks).reshape((-1,) + (1,) * (len(extent) - axis_at - 1))

    loudness = one(*pieces[0])
    for cut in pieces[1:]:
        loudness = loudness * one(*cut)
    return loudness


def centred(stream_key, dims, spread, limit, cuts=(), kind=jnp.bfloat16):
    entries = spread * jax.random.normal(stream_key, dims, jnp.float32)
    if cuts:
        entries = entries * steps_of(stream_key, dims, cuts, -0.22, 0.18)
    return jnp.clip(entries, -limit, limit).astype(kind)


def setup_inputs(seed: int = 0) -> dict:
    key_list = jax.random.split(jax.random.key(seed), 8)
    anchors = centred(key_list[0], (ANCHORS, W), 1.0, 6.0, ((0, 32),))
    coefs = centred(key_list[1], (NRB, BLK, SLOTS * BLK), (SLOTS * BLK) ** -0.5, 0.1875, ((0, 512),))
    block_cols = draw_block_cols(jax.random.fold_in(key_list[7], 71), 0)
    block_counts = draw_block_counts(jax.random.fold_in(key_list[7], 71), 0)
    sample_rows = set_ends(jax.random.randint(key_list[4], (BATCH, F), 0, ROWS_DEV), jax.random.fold_in(key_list[4], 1), 0, ROWS_DEV - 1).astype(jnp.int32)
    labels = set_ends((jax.random.randint(key_list[5], (BATCH,), 0, 2) < 1).astype(jnp.int32), jax.random.fold_in(key_list[5], 1), 0, 1)
    pair_weights = centred(key_list[6], (F, F), 0.01, 0.06, (), jnp.float32)
    return {"anchors": anchors, "coefs": coefs, "block_cols": block_cols, "block_counts": block_counts, "sample_rows": sample_rows, "labels": labels, "pair_weights": pair_weights}


def one_step(anchors, coefs, block_cols, live, sample_rows, labels, sym):
    blocks = anchors.reshape(BLOCKS, BLK, W)
    devices = block_cols.shape[0] // RB_DEV

    def device_step(carry, index):
        cols = lax.dynamic_slice_in_dim(block_cols, index * RB_DEV, RB_DEV, 0)
        alive = lax.dynamic_slice_in_dim(live, index * RB_DEV, RB_DEV, 0)
        coef = lax.dynamic_slice_in_dim(coefs, index * RB_DEV, RB_DEV, 0)
        stacked = blocks[cols] * alive[:, :, None, None].astype(jnp.bfloat16)
        stacked = stacked.reshape(RB_DEV, SLOTS * BLK, W)
        table = jnp.einsum("rik,rkw->riw", coef.astype(jnp.float32), stacked.astype(jnp.float32))
        table = table.astype(jnp.bfloat16).reshape(ROWS_DEV, W)
        rows = lax.dynamic_slice_in_dim(sample_rows, index * SMP_DEV, SMP_DEV, 0)
        target = lax.dynamic_slice_in_dim(labels, index * SMP_DEV, SMP_DEV, 0).astype(jnp.float32)
        vecs = table[rows].astype(jnp.float32)
        proj = jnp.einsum("fg,sgw->sfw", sym.astype(jnp.float32), vecs)
        score = 0.5 * jnp.sum(vecs * proj, axis=(1, 2))
        slope = jax.nn.sigmoid(score) - target
        dvec = (slope[:, None, None] * proj).astype(jnp.bfloat16)
        row_grad = jax.ops.segment_sum(dvec.reshape(-1, W).astype(jnp.float32), rows.reshape(-1), num_segments=ROWS_DEV)
        row_grad = row_grad.astype(jnp.bfloat16).reshape(RB_DEV, BLK, W)
        slot_grads = jnp.einsum("rik,riw->rkw", coef.astype(jnp.float32), row_grad.astype(jnp.float32))
        slot_grads = slot_grads.reshape(RB_DEV, SLOTS, BLK, W) * alive[:, :, None, None].astype(jnp.float32)
        carry = carry.at[cols.reshape(-1)].add(slot_grads.reshape(RB_DEV * SLOTS, BLK * W))
        return carry, score

    start = jnp.zeros((BLOCKS, BLK * W), jnp.float32)
    grad, scores = lax.scan(device_step, start, jnp.arange(devices, dtype=jnp.int32))
    return grad.reshape(ANCHORS, W), scores.reshape(-1)


def reference(anchors, coefs, block_cols, block_counts, sample_rows, labels, pair_weights):
    live = (jnp.arange(SLOTS, dtype=jnp.int32)[None, :] < block_counts[:, None]).astype(jnp.int32)
    off = pair_weights * (1.0 - jnp.eye(F, dtype=jnp.float32))
    sym = (off + off.T).astype(jnp.bfloat16)
    grad_first, _ = one_step(anchors, coefs, block_cols, live, sample_rows, labels, sym)
    next_anchors = (anchors.astype(jnp.float32) - grad_first).astype(jnp.bfloat16)
    grad_second, scores = one_step(next_anchors, coefs, block_cols, live, sample_rows, labels, sym)
    update = -(grad_first + grad_second)
    return update, scores
```

```python
import functools

import jax
import jax.numpy as jnp
from jax import lax
from jax.experimental import pallas as pl
from jax.experimental.pallas import tpu as pltpu
from jax.sharding import PartitionSpec as P

BF = jnp.bfloat16
F32 = jnp.float32
HIGH = lax.Precision.HIGHEST
MESH = pl.DeviceIdType.MESH
VMEM = pltpu.VMEM
DMA = pltpu.SemaphoreType.DMA
UNROLL = 8


def dot(a, b, dims=((1,), (0,)), precision=None):
    return lax.dot_general(a, b, (dims, ((), ())), precision=precision, preferred_element_type=F32)


def split(x):
    high = x.astype(BF)
    return high, (x - high.astype(F32)).astype(BF)


def call(body, outs, scratch, collective_id=None, limit=32 << 20):
    params = {} if collective_id is None else {"collective_id": collective_id, "has_side_effects": True}
    return pl.pallas_call(
        body,
        out_shape=outs,
        scratch_shapes=scratch,
        compiler_params=pltpu.CompilerParams(vmem_limit_bytes=limit, **params),
    )


def plane_place():
    return lax.axis_index("group") * 2 + lax.axis_index("dev") % 2, lax.axis_index("dev") // 2


def plane_device(place, z):
    return {"group": place // 2, "dev": z * 2 + place % 2}


def plane_barrier(size):
    me, z = plane_place()
    barrier = pltpu.get_barrier_semaphore()

    def greet(j, carry):
        pl.semaphore_signal(barrier, inc=1, device_id=plane_device((me + j) % size, z), device_id_type=MESH)
        return carry

    lax.fori_loop(1, size, greet, 0)
    pl.semaphore_wait(barrier, size - 1)


def plane_copy(size, j, source, target, send_sem, recv_sem):
    me, z = plane_place()
    partner = (me + j) % size
    return pltpu.make_async_remote_copy(
        src_ref=source(partner),
        dst_ref=target.at[me],
        send_sem=send_sem.at[j],
        recv_sem=recv_sem.at[j],
        device_id=plane_device(partner, z),
        device_id_type=MESH,
    )


def plane_start(size, source, target, send_sem, recv_sem):
    def start(j, carry):
        plane_copy(size, j, source, target, send_sem, recv_sem).start()
        return carry

    lax.fori_loop(1, size, start, 0)


def plane_wait(size, source, target, send_sem, recv_sem):
    def wait(j, carry):
        plane_copy(size, j, source, target, send_sem, recv_sem).wait()
        return carry

    lax.fori_loop(1, size, wait, 0)


def ring_barrier(length):
    dev = lax.axis_index("dev")
    barrier = pltpu.get_barrier_semaphore()
    for step in (2, length * 2 - 2):
        pl.semaphore_signal(
            barrier, inc=1, device_id={"dev": (dev + step) % (length * 2)}, device_id_type=MESH
        )
    pl.semaphore_wait(barrier, 2)


def begin_kernel(size, anchors_ref, ids_ref, mine_ref, all_ref, out_buf, send_sem, recv_sem, pair_sems):
    me, z = plane_place()
    dev = lax.axis_index("dev")
    core = dev % 2
    half = mine_ref.shape[2]
    plane_barrier(size)
    plane_start(size, lambda partner: ids_ref, all_ref, send_sem, recv_sem)
    all_ref[me] = ids_ref[...]
    anchors = anchors_ref[...]
    total = anchors.shape[0]
    rows = 2 * half
    blk = total // half
    row = lax.broadcasted_iota(jnp.int32, (rows, total), 0)
    col = lax.broadcasted_iota(jnp.int32, (rows, total), 1)

    def pick(place):
        wanted = (row % half) * blk + place * 2 + row // half
        return dot(jnp.where(col == wanted, 1.0, 0.0).astype(BF), anchors).astype(BF)

    out_buf[...] = pick(me + 1 - 2 * core).reshape(out_buf.shape)
    pair = pltpu.make_async_remote_copy(
        src_ref=out_buf,
        dst_ref=mine_ref.at[core],
        send_sem=pair_sems.at[0],
        recv_sem=pair_sems.at[1],
        device_id={"dev": dev + 1 - 2 * core},
        device_id_type=MESH,
    )
    pair.start()
    mine_ref[core] = pick(me).reshape(out_buf.shape)
    pair.wait()
    plane_wait(size, lambda partner: ids_ref, all_ref, send_sem, recv_sem)


def ring_gather_kernel(length, mine_ref, out_ref, send_sem, recv_sem):
    dev = lax.axis_index("dev")
    z = dev // 2
    ring_barrier(length)
    out_ref[z] = mine_ref[...]
    steps = (length // 2, length - 1 - length // 2)

    def copy(way, t):
        sign = 1 if way == 0 else -1
        chunk = (z - sign * t + length) % length
        return pltpu.make_async_remote_copy(
            src_ref=mine_ref if t == 0 else out_ref.at[chunk],
            dst_ref=out_ref.at[chunk],
            send_sem=send_sem.at[way, t],
            recv_sem=recv_sem.at[way, t],
            device_id={"dev": (dev + sign * 2 + 2 * length) % (2 * length)},
            device_id_type=MESH,
        )

    sent = []
    for t in range(max(steps)):
        for way in (0, 1):
            if t < steps[way]:
                if t:
                    copy(way, t - 1).wait_recv()
                moved = copy(way, t)
                moved.start()
                sent.append(moved)
    for way in (0, 1):
        copy(way, steps[way] - 1).wait_recv()
    for moved in sent:
        moved.wait_send()


def forward_kernel(size, picker_ref, every_ref, weights_ref, table_ref, out_buf, in_buf, send_sem, recv_sem):
    me, z = plane_place()
    _, pair, span, width = out_buf.shape
    picker = picker_ref[...]
    for i in range(pair):
        picked = dot(picker, every_ref[:, i].reshape(-1, width)).astype(BF)
        out_buf[:, i] = picked.reshape(size, span, width)
    plane_barrier(size)
    plane_start(size, lambda partner: out_buf.at[partner], in_buf, send_sem, recv_sem)
    in_buf[me] = out_buf[me]
    plane_wait(size, lambda partner: out_buf.at[partner], in_buf, send_sem, recv_sem)
    table_ref[...] = dot(weights_ref[...], in_buf[...].reshape(-1, width)).astype(BF)


def interact_kernel(table_ref, ids_ref, labels_ref, mix_ref, rg_ref, score_ref, ot_ref, pt_ref, z_ref):
    rows, width = table_ref.shape
    chunks, lanes = ids_ref.shape
    per = labels_ref.shape[1]
    fields = lanes // per
    mix = mix_ref[...]
    row_iota = lax.broadcasted_iota(jnp.int32, (rows, lanes), 0)
    table = table_ref[...]
    gram_high, gram_low = split(dot(table, table, ((1,), (1,))))
    gram = jnp.concatenate([gram_high, gram_low], axis=0)

    def first(step, carry):
        for u in range(UNROLL):
            c = step * UNROLL + u
            ot = jnp.where(row_iota == ids_ref[pl.ds(c, 1), :], 1.0, 0.0).astype(BF)
            ot_ref[c] = ot
            pt = dot(ot, mix).astype(BF)
            pt_ref[c] = pt
            q = dot(gram, ot)
            q = q[:rows] + q[rows:]
            z_ref[pl.ds(c, 1), :] = jnp.sum(q * pt.astype(F32), axis=0, keepdims=True)
        return carry

    lax.fori_loop(0, chunks // UNROLL, first, 0)
    member = jnp.where(
        lax.broadcasted_iota(jnp.int32, (lanes, per), 0) // fields
        == lax.broadcasted_iota(jnp.int32, (lanes, per), 1),
        1.0,
        0.0,
    ).astype(F32)
    score = 0.5 * dot(z_ref[...], member, precision=HIGH)
    score_ref[...] = score
    slope = 1.0 / (1.0 + jnp.exp(-score)) - labels_ref[...].astype(F32)
    z_ref[...] = dot(slope, member, ((1,), (1,)), precision=HIGH)

    def second(step, total):
        for u in range(UNROLL):
            c = step * UNROLL + u
            w = (z_ref[pl.ds(c, 1), :] * pt_ref[c].astype(F32)).astype(BF)
            total = total + dot(w, ot_ref[c], ((1,), (1,)))
        return total

    total = lax.fori_loop(0, chunks // UNROLL, second, jnp.zeros((rows, rows), F32))
    high, low = split(total)
    rg_ref[...] = (dot(high, table) + dot(low, table)).astype(BF)


def backward_kernel(size, weights_ref, rg_ref, placer_ref, sums_ref, out_buf, in_buf, send_sem, recv_sem):
    me, z = plane_place()
    _, pair, span, width = out_buf.shape
    out_buf[...] = dot(weights_ref[...], rg_ref[...]).astype(BF).reshape(out_buf.shape)
    plane_barrier(size)
    plane_start(size, lambda partner: out_buf.at[partner], in_buf, send_sem, recv_sem)
    in_buf[me] = out_buf[me]
    plane_wait(size, lambda partner: out_buf.at[partner], in_buf, send_sem, recv_sem)
    placer = placer_ref[...]
    for i in range(pair):
        summed = dot(placer, in_buf[:, i].reshape(-1, width))
        sums_ref[:, i] = summed.reshape(sums_ref.shape[0], -1, width)


def ring_reduce_kernel(length, sums_ref, mine_ref, past_ref, grad_ref, next_ref, out_buf, in_buf, send_sem, recv_sem):
    dev = lax.axis_index("dev")
    z = dev // 2
    ring_barrier(length)
    steps = (length // 2, length - 1 - length // 2)

    def copy(way, t):
        sign = 1 if way == 0 else -1
        return pltpu.make_async_remote_copy(
            src_ref=out_buf.at[way, t],
            dst_ref=in_buf.at[way, t],
            send_sem=send_sem.at[way, t],
            recv_sem=recv_sem.at[way, t],
            device_id={"dev": (dev + sign * 2 + 2 * length) % (2 * length)},
            device_id_type=MESH,
        )

    sent = []
    for t in range(max(steps)):
        for way in (0, 1):
            if t < steps[way]:
                sign = 1 if way == 0 else -1
                chunk = (z + sign * (steps[way] - t) + length) % length
                value = sums_ref[chunk]
                if t:
                    copy(way, t - 1).wait_recv()
                    value = value + in_buf[way, t - 1].astype(F32)
                out_buf[way, t] = value.astype(BF)
                moved = copy(way, t)
                moved.start()
                sent.append(moved)
    grad = sums_ref[z]
    for way in (0, 1):
        copy(way, steps[way] - 1).wait_recv()
        grad = grad + in_buf[way, steps[way] - 1].astype(F32)
    grad_ref[...] = grad + past_ref[...]
    next_ref[...] = (mine_ref[...].astype(F32) - grad).astype(BF)
    for moved in sent:
        moved.wait_send()


def finish_kernel(size, grad_ref, update_ref, out_buf, in_buf, send_sem, recv_sem):
    me, z = plane_place()
    _, pair, half, width = in_buf.shape
    out_buf[0] = (-grad_ref[:, :half]).astype(BF)
    out_buf[1] = (-grad_ref[:, half:]).astype(BF)
    plane_barrier(size)
    plane_start(size, lambda partner: out_buf.at[partner % 2], in_buf, send_sem, recv_sem)
    in_buf[me] = out_buf[me % 2]
    total = size * pair * half
    source = lax.broadcasted_iota(jnp.int32, (1, total), 1)
    place = (source % half) * (size * pair) + source // half
    row = lax.broadcasted_iota(jnp.int32, (total, total), 0)
    order = jnp.where(row == place, 1.0, 0.0).astype(BF)
    plane_wait(size, lambda partner: out_buf.at[partner % 2], in_buf, send_sem, recv_sem)
    update_ref[...] = dot(order, in_buf[...].reshape(total, width))


def per_device(anchors, coefs, block_cols, block_counts, sample_rows, labels, pair_weights):
    length = lax.axis_size("dev") // 2
    size = lax.axis_size("group") * 2
    rblocks, slots = block_cols.shape
    blk = coefs.shape[1]
    width = anchors.shape[1]
    own = anchors.shape[0] // blk
    span = rblocks * slots
    blocks = length * 2 * own
    pair = blk // size
    rows = rblocks * blk

    live = (jnp.arange(slots)[None, :] < block_counts[:, None]).astype(BF)
    masked = coefs.reshape(rblocks, blk, slots, size, pair) * live[:, None, :, None, None]
    spread = masked[:, :, None] * jnp.eye(rblocks, dtype=BF)[:, None, :, None, None, None]
    weights = spread.transpose(0, 1, 4, 5, 2, 3).reshape(rows, size * pair * span)

    fields = pair_weights.shape[0]
    off = pair_weights * (1.0 - jnp.eye(fields, dtype=F32))
    sym = (off + off.T).astype(BF)
    per = 256 // fields
    mix = jnp.kron(jnp.eye(per, dtype=BF), sym)
    row_ids = sample_rows.reshape(-1, per * fields)
    targets = labels.reshape(-1, per)
    chunks, lanes = row_ids.shape

    def shape(dims, kind=BF):
        return jax.ShapeDtypeStruct(dims, kind)

    sems = [DMA((size,)), DMA((size,))]
    ring_sems = [DMA((2, length // 2)), DMA((2, length // 2))]
    plane_buf = VMEM((size, pair, span, width), BF)

    ids_tile = jnp.broadcast_to(
        jnp.pad(block_cols.reshape(1, span), ((0, 0), (0, 128 - span))), (8, 128)
    )
    mine, all_ids = call(
        functools.partial(begin_kernel, size),
        (shape((2, pair, own, width)), shape((size, 8, 128), jnp.int32)),
        [VMEM((pair, own, width), BF)] + sems + [DMA((2,))],
        0,
    )(anchors, ids_tile)
    mine = mine.transpose(1, 0, 2, 3).reshape(pair, 2 * own, width)
    ids = all_ids[:, 0, :span].reshape(size * span)
    picker = (ids[:, None] == jnp.arange(blocks)[None, :]).astype(BF)
    placer = (ids[None, :] == jnp.arange(blocks)[:, None]).astype(BF)
    weights_t = weights.T

    def one_step(mine, past):
        every = call(
            functools.partial(ring_gather_kernel, length),
            shape((length, pair, 2 * own, width)),
            ring_sems,
            1,
        )(mine)
        table = call(
            functools.partial(forward_kernel, size), shape((rows, width)), [plane_buf, plane_buf] + sems, 2
        )(picker, every, weights)
        row_grad, score = call(
            interact_kernel,
            (shape((rows, width)), shape(targets.shape, F32)),
            [VMEM((chunks, rows, lanes), BF), VMEM((chunks, rows, lanes), BF), VMEM((chunks, lanes), F32)],
        )(table, row_ids, targets, mix)
        sums = call(
            functools.partial(backward_kernel, size),
            shape((length, pair, 2 * own, width), F32),
            [plane_buf, plane_buf] + sems,
            3,
        )(weights_t, row_grad, placer)
        ring_buf = VMEM((2, length // 2, pair, 2 * own, width), BF)
        grad, following = call(
            functools.partial(ring_reduce_kernel, length),
            (shape(mine.shape, F32), shape(mine.shape)),
            [ring_buf, ring_buf] + ring_sems,
            4,
        )(sums, mine, past)
        return grad, following, score

    grad, following, _ = one_step(mine, jnp.zeros(mine.shape, F32))
    grad, _, score = one_step(following, grad)
    update = call(
        functools.partial(finish_kernel, size),
        shape(anchors.shape, F32),
        [VMEM((2, pair, own, width), BF), VMEM((size, pair, own, width), BF)] + sems,
        5,
    )(grad)
    return update, score.reshape(-1)


def solution(mesh):
    return jax.shard_map(
        per_device,
        mesh=mesh,
        in_specs=(
            P("dev", None),
            P(("group", "dev"), None, None),
            P(("group", "dev"), None),
            P(("group", "dev")),
            P(("group", "dev"), None),
            P(("group", "dev")),
            P(),
        ),
        out_specs=(P("dev", None), P(("group", "dev"))),
        check_vma=False,
    )
```

```python
import functools

import jax
import jax.numpy as jnp
from jax import lax
from jax.experimental import pallas as pl
from jax.experimental.pallas import tpu as pltpu
from jax.sharding import PartitionSpec as P

BF = jnp.bfloat16
F32 = jnp.float32
HIGH = lax.Precision.HIGHEST
MESH = pl.DeviceIdType.MESH
VMEM = pltpu.VMEM
DMA = pltpu.SemaphoreType.DMA
UNROLL = 8
NEAR = (1, -1, 2, -2)
FAR = 5
STEPS = 2
PART = 8


def dot(a, b, dims=((1,), (0,)), precision=None):
    return lax.dot_general(a, b, (dims, ((), ())), precision=precision, preferred_element_type=F32)


def split(x):
    high = x.astype(BF)
    return high, (x - high.astype(F32)).astype(BF)


def whole_kernel(
    size,
    length,
    anchors_ref,
    ids_ref,
    weights_ref,
    weights_t_ref,
    rows_ref,
    labels_ref,
    mix_ref,
    update_ref,
    score_ref,
    mine,
    pair_out,
    all_ids,
    every,
    placer,
    picker,
    ot_buf,
    pt_buf,
    z_buf,
    table_buf,
    fore_out,
    fore_in,
    back_out,
    back_in,
    acc_buf,
    sums,
    reduce_in,
    half_in,
    collect_out,
    total_buf,
    last_out,
    last_in,
    ids_sems,
    fore_sems,
    back_sems,
    last_sems,
    gather_sems,
    reduce_sems,
    pair_sems,
):
    group, dev = lax.axis_index("group"), lax.axis_index("dev")
    core, z = dev % 2, dev // 2
    me = group * 2 + core
    parts = size // PART
    _, pair, own, width = mine.shape
    span = fore_out.shape[2]
    blocks = placer.shape[0]
    rows = table_buf.shape[0]
    chunks, lanes = rows_ref.shape
    per = labels_ref.shape[1]
    fields = lanes // per

    def partner_of(n):
        return ((me // PART + n // PART) % parts) * PART + (me % PART + n % PART) % PART

    def plane_copy(n, source, target, sems):
        partner = partner_of(n)
        return pltpu.make_async_remote_copy(
            src_ref=source(partner),
            dst_ref=target.at[me],
            send_sem=sems.at[0, n],
            recv_sem=sems.at[1, n],
            device_id={"group": partner // 2, "dev": z * 2 + partner % 2},
            device_id_type=MESH,
        )

    def plane_each(first, last, act, source, target, sems):
        def one(n, carry):
            act(plane_copy(n, source, target, sems))
            return carry

        lax.fori_loop(first, last, one, 0)

    def start(copy):
        copy.start()

    def wait_recv(copy):
        copy.wait_recv()

    def wait_send(copy):
        copy.wait_send()

    def ring_device(s):
        return {"dev": (dev + 2 * s + 2 * length) % (2 * length)}

    def ring_copy(n, s, source, target, sems):
        return pltpu.make_async_remote_copy(
            src_ref=source,
            dst_ref=target,
            send_sem=sems.at[0, n],
            recv_sem=sems.at[1, n],
            device_id=ring_device(s),
            device_id_type=MESH,
        )

    barrier = pltpu.get_barrier_semaphore()

    def greet(n, carry):
        partner = partner_of(n)
        pl.semaphore_signal(
            barrier,
            inc=1,
            device_id={"group": partner // 2, "dev": z * 2 + partner % 2},
            device_id_type=MESH,
        )
        return carry

    lax.fori_loop(1, size, greet, 0)
    ring_mates = NEAR + (3, -3, FAR, -FAR)
    for s in ring_mates:
        pl.semaphore_signal(barrier, inc=1, device_id=ring_device(s), device_id_type=MESH)

    anchors = anchors_ref[...]
    held = anchors.shape[0]
    blk = held // own
    row = lax.broadcasted_iota(jnp.int32, (pair * own, held), 0)
    col = lax.broadcasted_iota(jnp.int32, (pair * own, held), 1)

    def pick(place):
        wanted = (row % own) * blk + place * pair + row // own
        return dot(jnp.where(col == wanted, 1.0, 0.0).astype(BF), anchors).astype(BF)

    pair_out[...] = pick(me + 1 - 2 * core).reshape(pair_out.shape)
    mine[core] = pick(me).reshape(pair_out.shape)
    pl.semaphore_wait(barrier, size - 1 + len(ring_mates))

    pair_copy = pltpu.make_async_remote_copy(
        src_ref=pair_out,
        dst_ref=mine.at[core],
        send_sem=pair_sems.at[0],
        recv_sem=pair_sems.at[1],
        device_id={"dev": dev + 1 - 2 * core},
        device_id_type=MESH,
    )
    pair_copy.start()
    own_ids = lambda partner: ids_ref
    plane_each(1, size, start, own_ids, all_ids, ids_sems)
    all_ids[me] = ids_ref[...]

    row_iota = lax.broadcasted_iota(jnp.int32, (rows, lanes), 0)
    mix = mix_ref[...]

    def prepare(step, carry):
        for u in range(UNROLL):
            c = step * UNROLL + u
            ot = jnp.where(row_iota == rows_ref[pl.ds(c, 1), :], 1.0, 0.0).astype(BF)
            ot_buf[c] = ot
            pt_buf[c] = dot(ot, mix).astype(BF)
        return carry

    member = jnp.where(
        lax.broadcasted_iota(jnp.int32, (lanes, per), 0) // fields
        == lax.broadcasted_iota(jnp.int32, (lanes, per), 1),
        1.0,
        0.0,
    ).astype(F32)
    total_buf[...] = jnp.zeros(total_buf.shape, F32)
    pair_copy.wait()

    def gather_start():
        zm, zp = (z + length - FAR) % length, (z + FAR) % length
        own_copies = [
            ring_copy(n, s, mine, every.at[z], gather_sems) for n, s in enumerate((FAR, -FAR) + NEAR)
        ]
        low = [ring_copy(6 + n, s, every.at[zm], every.at[zm], gather_sems) for n, s in enumerate(NEAR)]
        low.append(ring_copy(10, 3, every.at[zm, 0], every.at[zm, 0], gather_sems))
        high = [ring_copy(11 + n, s, every.at[zp], every.at[zp], gather_sems) for n, s in enumerate(NEAR)]
        high.append(ring_copy(15, -3, every.at[zp, 1], every.at[zp, 1], gather_sems))
        for copy in own_copies:
            copy.start()
        every[z] = mine[...]
        return own_copies, low, high

    def gather_end(own_copies, low, high):
        own_copies[0].wait_recv()
        for copy in low:
            copy.start()
        own_copies[1].wait_recv()
        for copy in high:
            copy.start()
        for copy in own_copies[2:] + low + high:
            copy.wait_recv()
        for copy in own_copies + low + high:
            copy.wait_send()

    def reduce():
        def near(k):
            return (z + k + 2 * length) % length

        copies = []
        for a, s in enumerate(NEAR):
            copies.append(ring_copy(a, s, sums.at[near(s - FAR)], reduce_in.at[a], reduce_sems))
            copies.append(ring_copy(4 + a, s, sums.at[near(s + FAR)], reduce_in.at[4 + a], reduce_sems))
        copies.append(ring_copy(8, -3, sums.at[near(8), 0], half_in.at[0], reduce_sems))
        copies.append(ring_copy(9, 3, sums.at[near(8), 1], half_in.at[1], reduce_sems))
        direct = [
            ring_copy(10 + a, s, sums.at[near(s)], reduce_in.at[8 + a], reduce_sems)
            for a, s in enumerate(NEAR)
        ]
        for copy in copies + direct:
            copy.start()
        for copy in copies:
            copy.wait_recv()
        far = []
        for h, s in ((0, -FAR), (1, FAR)):
            value = sums[near(s)].astype(F32)
            for a in range(4):
                value = value + reduce_in[4 * h + a].astype(F32)
            collect_out[h, 1 - h] = value[1 - h].astype(BF)
            collect_out[h, h] = (value[h] + half_in[h].astype(F32)).astype(BF)
            far.append(ring_copy(14 + h, s, collect_out.at[h], reduce_in.at[12 + h], reduce_sems))
            far[h].start()
        grad = sums[z].astype(F32)
        for a, copy in enumerate(direct):
            copy.wait_recv()
            grad = grad + reduce_in[8 + a].astype(F32)
        for h, copy in enumerate(far):
            copy.wait_recv()
            grad = grad + reduce_in[12 + h].astype(F32)
        for copy in copies + direct + far:
            copy.wait_send()
        return grad

    fore_source = lambda partner: fore_out.at[partner]
    back_source = lambda partner: back_out.at[partner]

    def part_of(q, sign):
        return (me // PART + sign * q + parts) % parts

    def forward():
        for q in range(parts):
            part = part_of(q, 1)
            picks = picker[pl.ds(pl.multiple_of(part * PART * span, PART * span), PART * span), :]
            for i in range(pair):
                picked = dot(picks, every[:, :, i].reshape(blocks, width)).astype(BF)
                fore_out[pl.ds(part * PART, PART), i] = picked.reshape(PART, span, width)
            plane_each(max(1, q * PART), (q + 1) * PART, start, fore_source, fore_in, fore_sems)
        fore_in[me] = fore_out[me]
        depth = PART * pair * span
        table = jnp.zeros((rows, width), F32)
        for q in range(parts):
            plane_each(max(1, q * PART), (q + 1) * PART, wait_recv, fore_source, fore_in, fore_sems)
            part = part_of(q, -1)
            weights = weights_ref[:, pl.ds(pl.multiple_of(part * depth, depth), depth)]
            table = table + dot(weights, fore_in[pl.ds(part * PART, PART)].reshape(depth, width))
        table_buf[...] = table.astype(BF)
        plane_each(1, size, wait_send, fore_source, fore_in, fore_sems)

    def interact():
        table = table_buf[...]
        gram_high, gram_low = split(dot(table, table, ((1,), (1,))))
        gram = jnp.concatenate([gram_high, gram_low], axis=0)

        def first(step, carry):
            for u in range(UNROLL):
                c = step * UNROLL + u
                q = dot(gram, ot_buf[c])
                q = q[:rows] + q[rows:]
                z_buf[pl.ds(c, 1), :] = jnp.sum(q * pt_buf[c].astype(F32), axis=0, keepdims=True)
            return carry

        lax.fori_loop(0, chunks // UNROLL, first, 0)
        score = 0.5 * dot(z_buf[...], member, precision=HIGH)
        score_ref[...] = score
        slope = 1.0 / (1.0 + jnp.exp(-score)) - labels_ref[...].astype(F32)
        z_buf[...] = dot(slope, member, ((1,), (1,)), precision=HIGH)

        def second(step, total):
            for u in range(UNROLL):
                c = step * UNROLL + u
                w = (z_buf[pl.ds(c, 1), :] * pt_buf[c].astype(F32)).astype(BF)
                total = total + dot(w, ot_buf[c], ((1,), (1,)))
            return total

        total = lax.fori_loop(0, chunks // UNROLL, second, jnp.zeros((rows, rows), F32))
        high, low = split(total)
        return (dot(high, table) + dot(low, table)).astype(BF)

    def backward(row_grad):
        depth = PART * pair * span
        for q in range(parts):
            part = part_of(q, 1)
            weights = weights_t_ref[pl.ds(pl.multiple_of(part * depth, depth), depth), :]
            back_out[pl.ds(part * PART, PART)] = (
                dot(weights, row_grad).astype(BF).reshape(PART, pair, span, width)
            )
            plane_each(max(1, q * PART), (q + 1) * PART, start, back_source, back_in, back_sems)
        back_in[me] = back_out[me]
        depth = PART * span
        for q in range(parts):
            plane_each(max(1, q * PART), (q + 1) * PART, wait_recv, back_source, back_in, back_sems)
            part = part_of(q, -1)
            places = placer[:, pl.ds(pl.multiple_of(part * depth, depth), depth)]
            for i in range(pair):
                value = dot(places, back_in[pl.ds(part * PART, PART), i].reshape(depth, width))
                if q:
                    value = value + acc_buf[i]
                if q < parts - 1:
                    acc_buf[i] = value
                else:
                    sums[:, :, i] = value.astype(BF).reshape(length, 2, own, width)
        plane_each(1, size, wait_send, back_source, back_in, back_sems)

    def one_step(step, carry):
        pending = gather_start()

        @pl.when(step == 0)
        def _():
            lax.fori_loop(0, chunks // UNROLL, prepare, 0)
            plane_each(1, size, wait_recv, own_ids, all_ids, ids_sems)
            plane_each(1, size, wait_send, own_ids, all_ids, ids_sems)
            quarter = lax.broadcasted_iota(jnp.int32, (1, 128), 1) // span
            block_iota = lax.broadcasted_iota(jnp.int32, (blocks, 128), 0)
            together = 128 // span
            for t in range(size // together):
                line = all_ids[t * together, 0:1, :]
                for u in range(1, together):
                    line = jnp.where(quarter == u, all_ids[t * together + u, 0:1, :], line)
                hot = jnp.where(block_iota == line, 1.0, 0.0)
                placer[:, t * 128 : (t + 1) * 128] = hot.astype(BF)
                picker[t * 128 : (t + 1) * 128, :] = hot.T.astype(BF)

        gather_end(*pending)
        forward()
        backward(interact())
        grad = reduce()
        total_buf[...] = total_buf[...] + grad
        mine[...] = (mine[...].astype(F32) - grad).astype(BF)
        return carry

    lax.fori_loop(0, STEPS, one_step, 0)

    last_out[...] = (-total_buf[...]).astype(BF)
    last_source = lambda partner: last_out.at[partner % 2]
    plane_each(1, size, start, last_source, last_in, last_sems)
    last_in[me] = last_out[core]
    source = lax.broadcasted_iota(jnp.int32, (1, held), 1)
    place = (source % own) * blk + source // own
    target = lax.broadcasted_iota(jnp.int32, (held, held), 0)
    order = jnp.where(target == place, 1.0, 0.0).astype(BF)
    plane_each(1, size, wait_recv, last_source, last_in, last_sems)
    update_ref[...] = dot(order, last_in[...].reshape(held, width))
    plane_each(1, size, wait_send, last_source, last_in, last_sems)


def per_device(anchors, coefs, block_cols, block_counts, sample_rows, labels, pair_weights):
    length = lax.axis_size("dev") // 2
    size = lax.axis_size("group") * 2
    rblocks, slots = block_cols.shape
    blk = coefs.shape[1]
    width = anchors.shape[1]
    own = anchors.shape[0] // blk
    span = rblocks * slots
    blocks = length * 2 * own
    pair = blk // size
    rows = rblocks * blk

    live = (jnp.arange(slots)[None, :] < block_counts[:, None]).astype(BF)
    masked = coefs.reshape(rblocks, blk, slots, size, pair) * live[:, None, :, None, None]
    spread = masked[:, :, None] * jnp.eye(rblocks, dtype=BF)[:, None, :, None, None, None]
    weights = spread.transpose(0, 1, 4, 5, 2, 3).reshape(rows, size * pair * span)

    fields = pair_weights.shape[0]
    off = pair_weights * (1.0 - jnp.eye(fields, dtype=F32))
    sym = (off + off.T).astype(BF)
    per = 256 // fields
    mix = jnp.kron(jnp.eye(per, dtype=BF), sym)
    row_ids = sample_rows.reshape(-1, per * fields)
    targets = labels.reshape(-1, per)
    chunks, lanes = row_ids.shape
    ids_tile = jnp.broadcast_to(jnp.tile(block_cols.reshape(1, span), (1, 128 // span)), (8, 128))

    chunk = (2, pair, own, width)
    plane_buf = VMEM((size, pair, span, width), BF)
    update, score = pl.pallas_call(
        functools.partial(whole_kernel, size, length),
        out_shape=(
            jax.ShapeDtypeStruct(anchors.shape, F32),
            jax.ShapeDtypeStruct(targets.shape, F32),
        ),
        scratch_shapes=[
            VMEM(chunk, BF),
            VMEM((pair, own, width), BF),
            VMEM((size, 8, 128), jnp.int32),
            VMEM((length,) + chunk, BF),
            VMEM((blocks, size * span), BF),
            VMEM((size * span, blocks), BF),
            VMEM((chunks, rows, lanes), BF),
            VMEM((chunks, rows, lanes), BF),
            VMEM((chunks, lanes), F32),
            VMEM((rows, width), BF),
            plane_buf,
            plane_buf,
            plane_buf,
            plane_buf,
            VMEM((pair, blocks, width), F32),
            VMEM((length,) + chunk, BF),
            VMEM((14,) + chunk, BF),
            VMEM((2, pair, own, width), BF),
            VMEM((2,) + chunk, BF),
            VMEM(chunk, F32),
            VMEM((2, pair, own, width), BF),
            VMEM((size, pair, own, width), BF),
            DMA((2, size)),
            DMA((2, size)),
            DMA((2, size)),
            DMA((2, size)),
            DMA((2, 16)),
            DMA((2, 16)),
            DMA((2,)),
        ],
        compiler_params=pltpu.CompilerParams(
            collective_id=0, has_side_effects=True, vmem_limit_bytes=40 << 20
        ),
    )(anchors, ids_tile, weights, weights.T, row_ids, targets, mix)
    return update, score.reshape(-1)


def solution(mesh):
    return jax.shard_map(
        per_device,
        mesh=mesh,
        in_specs=(
            P("dev", None),
            P(("group", "dev"), None, None),
            P(("group", "dev"), None),
            P(("group", "dev")),
            P(("group", "dev"), None),
            P(("group", "dev")),
            P(),
        ),
        out_specs=(P("dev", None), P(("group", "dev"))),
        check_vma=False,
    )
```

```python
import functools

import jax
import jax.numpy as jnp
from jax import lax
from jax.experimental import pallas as pl
from jax.experimental.pallas import tpu as pltpu
from jax.sharding import PartitionSpec as P

BF = jnp.bfloat16
F32 = jnp.float32
HIGH = lax.Precision.HIGHEST
MESH = pl.DeviceIdType.MESH
VMEM = pltpu.VMEM
DMA = pltpu.SemaphoreType.DMA
UNROLL = 8
NEAR = (1, -1, 2, -2)
FAR = 5
STEPS = 2
PART = 8


def dot(a, b, dims=((1,), (0,)), precision=None):
    return lax.dot_general(a, b, (dims, ((), ())), precision=precision, preferred_element_type=F32)


def split(x):
    high = x.astype(BF)
    return high, (x - high.astype(F32)).astype(BF)


def whole_kernel(
    size,
    length,
    counts_ref,
    anchors_ref,
    coefs_ref,
    cols_ref,
    rows_ref,
    labels_ref,
    pairs_ref,
    update_ref,
    score_ref,
    mine,
    pair_out,
    ids_out,
    all_ids,
    every,
    placer,
    picker,
    weights,
    weights_t,
    rows_buf,
    ot_buf,
    pt_buf,
    z_buf,
    table_buf,
    fore_out,
    fore_in,
    back_out,
    back_in,
    acc_buf,
    sums,
    reduce_in,
    half_in,
    collect_out,
    total_buf,
    last_out,
    last_in,
    fore_sems,
    back_sems,
    gather_sems,
    reduce_sems,
    pair_sems,
):
    group, dev = lax.axis_index("group"), lax.axis_index("dev")
    core, z = dev % 2, dev // 2
    me = group * 2 + core
    parts = size // PART
    pair, _, own, width = mine.shape
    span = fore_out.shape[2]
    blocks = placer.shape[0]
    rows = table_buf.shape[0]
    rblocks, blk, deep = coefs_ref.shape
    slots = deep // blk
    chunks, lanes = rows_buf.shape
    per = labels_ref.shape[1]
    fields = lanes // per

    def iota(shape, dim):
        return lax.broadcasted_iota(jnp.int32, shape, dim)

    def hot(mask):
        return jnp.where(mask, 1.0, 0.0).astype(BF)

    def partner_of(n):
        return ((me // PART + n // PART) % parts) * PART + (me % PART + n % PART) % PART

    def plane_device(partner):
        return {"group": partner // 2, "dev": z * 2 + partner % 2}

    def plane_copy(n, i, source, target, sems):
        partner = partner_of(n)
        return pltpu.make_async_remote_copy(
            src_ref=source(partner),
            dst_ref=target.at[me],
            send_sem=sems.at[0, i * size + n],
            recv_sem=sems.at[1, i * size + n],
            device_id=plane_device(partner),
            device_id_type=MESH,
        )

    def plane_each(first, last, act, i, source, target, sems):
        def one(n, carry):
            act(plane_copy(n, i, source, target, sems))
            return carry

        lax.fori_loop(first, last, one, 0)

    def start(copy):
        copy.start()

    def wait_recv(copy):
        copy.wait_recv()

    def wait_send(copy):
        copy.wait_send()

    def ring_device(s):
        return {"dev": (dev + 2 * s + 2 * length) % (2 * length)}

    def ring_copy(n, i, s, source, target, sems):
        return pltpu.make_async_remote_copy(
            src_ref=source,
            dst_ref=target,
            send_sem=sems.at[0, i * 16 + n],
            recv_sem=sems.at[1, i * 16 + n],
            device_id=ring_device(s),
            device_id_type=MESH,
        )

    def near(k):
        return (z + k + 2 * length) % length

    barrier = pltpu.get_barrier_semaphore()

    def greet(n, carry):
        pl.semaphore_signal(
            barrier, inc=1, device_id=plane_device(partner_of(n)), device_id_type=MESH
        )
        return carry

    ring_mates = NEAR + (3, -3, FAR, -FAR)
    for s in ring_mates:
        pl.semaphore_signal(barrier, inc=1, device_id=ring_device(s), device_id_type=MESH)
    lax.fori_loop(1, size, greet, 0)

    anchors = anchors_ref[...]
    held = anchors.shape[0]
    row = iota((pair * own, held), 0)
    col = iota((pair * own, held), 1)

    def pick(place):
        wanted = (row % own) * blk + place * pair + row // own
        return dot(hot(col == wanted), anchors).astype(BF).reshape(pair_out.shape)

    pair_out[...] = pick(me + 1 - 2 * core)
    kept = pick(me)
    for i in range(pair):
        mine[i, core] = kept[i]
    line = jnp.concatenate([cols_ref[b : b + 1, :] for b in range(rblocks)] * (128 // span), axis=1)
    ids_out[...] = jnp.broadcast_to(line, ids_out.shape)
    pl.semaphore_wait(barrier, size - 1 + len(ring_mates))

    pair_copies = [
        pltpu.make_async_remote_copy(
            src_ref=pair_out.at[i],
            dst_ref=mine.at[i, core],
            send_sem=pair_sems.at[0, i],
            recv_sem=pair_sems.at[1, i],
            device_id={"dev": dev + 1 - 2 * core},
            device_id_type=MESH,
        )
        for i in range(pair)
    ]
    for copy in pair_copies:
        copy.start()
    own_ids = lambda partner: ids_out
    plane_each(1, size, start, 0, own_ids, all_ids, back_sems)
    all_ids[me] = ids_out[...]

    def gather_own(i):
        return [
            ring_copy(n, i, s, mine.at[i], every.at[i, z], gather_sems)
            for n, s in enumerate((FAR, -FAR) + NEAR)
        ]

    def gather_on(i, h):
        held_at = near(-FAR if h == 0 else FAR)
        piece = every.at[i, held_at]
        copies = [ring_copy(6 + 5 * h + n, i, s, piece, piece, gather_sems) for n, s in enumerate(NEAR)]
        half = every.at[i, held_at, h]
        copies.append(ring_copy(10 + 5 * h, i, 3 if h == 0 else -3, half, half, gather_sems))
        return copies

    def gather_start(i):
        for copy in gather_own(i):
            copy.start()
        every[i, z] = mine[i]

    def gather_forward(i):
        for h in (0, 1):
            gather_own(i)[h].wait_recv()
            for copy in gather_on(i, h):
                copy.start()

    def gather_end(i):
        for copy in gather_own(i)[2:] + gather_on(i, 0) + gather_on(i, 1):
            copy.wait_recv()

    def gather_sent():
        for i in range(pair):
            for copy in gather_own(i) + gather_on(i, 0) + gather_on(i, 1):
                copy.wait_send()

    for i in range(pair):
        pair_copies[i].wait()
        gather_start(i)

    member = jnp.where(
        iota((lanes, per), 0) // fields == iota((lanes, per), 1), 1.0, 0.0
    ).astype(F32)
    total_buf[...] = jnp.zeros(total_buf.shape, F32)
    off = jnp.where(iota((fields, fields), 0) == iota((fields, fields), 1), 0.0, pairs_ref[...])
    sym = (off + off.T).astype(BF)
    repeat = hot(iota((lanes, fields), 0) % fields == iota((lanes, fields), 1))
    mix = dot(dot(repeat, sym).astype(BF), repeat, ((1,), (1,)))
    mix = jnp.where(iota((lanes, lanes), 0) // fields == iota((lanes, lanes), 1) // fields, mix, 0.0)
    mix = mix.astype(BF)
    rows_buf[...] = jnp.concatenate(
        [rows_ref[pl.ds(u, chunks, stride=per), :] for u in range(per)], axis=1
    )
    row_iota = iota((rows, lanes), 0)

    def prepare(step, carry):
        for u in range(UNROLL):
            c = step * UNROLL + u
            ot = hot(row_iota == rows_buf[pl.ds(c, 1), :])
            ot_buf[c] = ot
            pt_buf[c] = dot(ot, mix).astype(BF)
        return carry

    lax.fori_loop(0, chunks // UNROLL, prepare, 0)
    for i in range(pair):
        gather_forward(i)

    plane_each(1, size, wait_recv, 0, own_ids, all_ids, back_sems)
    plane_each(1, size, wait_send, 0, own_ids, all_ids, back_sems)
    quarter = iota((1, 128), 1) // span
    block_iota = iota((blocks, 128), 0)
    together = 128 // span
    for t in range(size // together):
        line = all_ids[t * together, 0:1, :]
        for u in range(1, together):
            line = jnp.where(quarter == u, all_ids[t * together + u, 0:1, :], line)
        found = jnp.where(block_iota == line, 1.0, 0.0)
        placer[:, t * 128 : (t + 1) * 128] = found.astype(BF)
        picker[t * 128 : (t + 1) * 128, :] = found.T.astype(BF)

    flat = coefs_ref[...].reshape(rows, deep)
    tile = 256
    for t in range(weights.shape[1] // tile):
        n = iota((1, tile), 1) + t * tile
        slot, block = n % slots, (n // slots) % rblocks
        offset = (n // span) % size * pair + n // (span * size)
        order = hot(iota((deep, tile), 0) == slot * blk + offset)
        bound = jnp.where(block == 0, counts_ref[0], counts_ref[1])
        block = jnp.where(slot < bound, block, rblocks)
        value = jnp.where(iota((rows, tile), 0) // blk == block, dot(flat, order), 0.0)
        weights[:, t * tile : (t + 1) * tile] = value.astype(BF)
        weights_t[t * tile : (t + 1) * tile, :] = value.T.astype(BF)

    def part_of(q, sign):
        return (me // PART + sign * q + parts) % parts

    depth = PART * span

    def from_part(base, part):
        return pl.ds(pl.multiple_of(base + part * depth, depth), depth)

    def fore(act, i, q):
        first, last = max(1, q * PART), (q + 1) * PART
        plane_each(first, last, act, i, lambda partner: fore_out.at[i, partner], fore_in.at[i], fore_sems)

    def back(act, i, q):
        first, last = max(1, q * PART), (q + 1) * PART
        plane_each(first, last, act, i, lambda partner: back_out.at[i, partner], back_in.at[i], back_sems)

    def final(act, i):
        plane_each(1, size, act, i, lambda partner: last_out.at[i, partner % 2], last_in.at[i], fore_sems)

    def forward():
        for i in range(pair):
            gather_end(i)
            for q in range(parts):
                part = part_of(q, 1)
                picks = picker[from_part(0, part), :]
                picked = dot(picks, every[i].reshape(blocks, width)).astype(BF)
                fore_out[i, pl.ds(part * PART, PART)] = picked.reshape(PART, span, width)
                fore(start, i, q)
            fore_in[i, me] = fore_out[i, me]
        gather_sent()
        table = jnp.zeros((rows, width), F32)
        for i in range(pair):
            for q in range(parts):
                fore(wait_recv, i, q)
                part = part_of(q, -1)
                got = fore_in[i, pl.ds(part * PART, PART)].reshape(depth, width)
                table = table + dot(weights[:, from_part(i * size * span, part)], got)
        table_buf[...] = table.astype(BF)

    def interact():
        table = table_buf[...]
        gram_high, gram_low = split(dot(table, table, ((1,), (1,))))
        gram = jnp.concatenate([gram_high, gram_low], axis=0)

        def first(step, carry):
            for u in range(UNROLL):
                c = step * UNROLL + u
                q = dot(gram, ot_buf[c])
                q = q[:rows] + q[rows:]
                z_buf[pl.ds(c, 1), :] = jnp.sum(q * pt_buf[c].astype(F32), axis=0, keepdims=True)
            return carry

        lax.fori_loop(0, chunks // UNROLL, first, 0)
        score = 0.5 * dot(z_buf[...], member, precision=HIGH)
        score_ref[...] = score
        slope = 1.0 / (1.0 + jnp.exp(-score)) - labels_ref[...].astype(F32)
        z_buf[...] = dot(slope, member, ((1,), (1,)), precision=HIGH)

        def second(step, total):
            for u in range(UNROLL):
                c = step * UNROLL + u
                w = (z_buf[pl.ds(c, 1), :] * pt_buf[c].astype(F32)).astype(BF)
                total = total + dot(w, ot_buf[c], ((1,), (1,)))
            return total

        total = lax.fori_loop(0, chunks // UNROLL, second, jnp.zeros((rows, rows), F32))
        high, low = split(total)
        return (dot(high, table) + dot(low, table)).astype(BF)

    def reduce_copies(i):
        held_sums, taken = sums.at[i], reduce_in.at[i]
        copies = []
        for a, s in enumerate(NEAR):
            copies.append(ring_copy(a, i, s, held_sums.at[near(s - FAR)], taken.at[a], reduce_sems))
            copies.append(ring_copy(4 + a, i, s, held_sums.at[near(s + FAR)], taken.at[4 + a], reduce_sems))
        copies.append(ring_copy(8, i, -3, held_sums.at[near(8), 0], half_in.at[i, 0], reduce_sems))
        copies.append(ring_copy(9, i, 3, held_sums.at[near(8), 1], half_in.at[i, 1], reduce_sems))
        direct = [
            ring_copy(10 + a, i, s, held_sums.at[near(s)], taken.at[8 + a], reduce_sems)
            for a, s in enumerate(NEAR)
        ]
        far = [
            ring_copy(14 + h, i, s, collect_out.at[i, h], taken.at[12 + h], reduce_sems)
            for h, s in ((0, -FAR), (1, FAR))
        ]
        return copies, direct, far

    def backward(row_grad):
        for i in range(pair):
            for q in range(parts):
                part = part_of(q, 1)
                value = dot(weights_t[from_part(i * size * span, part), :], row_grad).astype(BF)
                back_out[i, pl.ds(part * PART, PART)] = value.reshape(PART, span, width)
                back(start, i, q)
            back_in[i, me] = back_out[i, me]
        for i in range(pair):
            for q in range(parts):
                fore(wait_send, i, q)
        for i in range(pair):
            for q in range(parts):
                back(wait_recv, i, q)
                part = part_of(q, -1)
                got = back_in[i, pl.ds(part * PART, PART)].reshape(depth, width)
                value = dot(placer[:, from_part(0, part)], got)
                if q:
                    value = value + acc_buf[...]
                if q < parts - 1:
                    acc_buf[...] = value
                else:
                    sums[i] = value.astype(BF).reshape(length, 2, own, width)
            copies, direct, _ = reduce_copies(i)
            for copy in copies + direct:
                copy.start()

    def collect(i):
        copies, _, far = reduce_copies(i)
        for copy in copies:
            copy.wait_recv()
        for h, s in ((0, -FAR), (1, FAR)):
            value = sums[i, near(s)].astype(F32)
            for a in range(4):
                value = value + reduce_in[i, 4 * h + a].astype(F32)
            collect_out[i, h, 1 - h] = value[1 - h].astype(BF)
            collect_out[i, h, h] = (value[h] + half_in[i, h].astype(F32)).astype(BF)
            far[h].start()

    def reduced(i):
        _, direct, far = reduce_copies(i)
        grad = sums[i, z].astype(F32)
        for copy in direct + far:
            copy.wait_recv()
        for a in range(6):
            grad = grad + reduce_in[i, 8 + a].astype(F32)
        return grad

    def one_step(step, carry):
        @pl.when(step > 0)
        def _():
            for i in range(pair):
                gather_forward(i)

        forward()
        backward(interact())
        for i in range(pair):
            collect(i)
        for i in range(pair):
            grad = reduced(i)
            total = total_buf[i] + grad
            total_buf[i] = total
            mine[i] = (mine[i].astype(F32) - grad).astype(BF)

            @pl.when(step < STEPS - 1)
            def _():
                gather_start(i)

            @pl.when(step == STEPS - 1)
            def _():
                last_out[i] = (-total).astype(BF)
                final(start, i)
                last_in[i, me] = last_out[i, core]

        for i in range(pair):
            copies, direct, far = reduce_copies(i)
            for copy in copies + direct + far:
                copy.wait_send()
            for q in range(parts):
                back(wait_send, i, q)
        return carry

    lax.fori_loop(0, STEPS, one_step, 0)

    source = iota((1, held), 1)
    place = (source % own) * blk + (source // own) % size * pair + source // (own * size)
    order = hot(iota((held, held), 0) == place)
    for i in range(pair):
        final(wait_recv, i)
    update_ref[...] = dot(order, last_in[...].reshape(held, width))
    for i in range(pair):
        final(wait_send, i)


def per_device(anchors, coefs, block_cols, block_counts, sample_rows, labels, pair_weights):
    length = lax.axis_size("dev") // 2
    size = lax.axis_size("group") * 2
    rblocks, slots = block_cols.shape
    blk = coefs.shape[1]
    width = anchors.shape[1]
    own = anchors.shape[0] // blk
    span = rblocks * slots
    blocks = length * 2 * own
    pair = blk // size
    rows = rblocks * blk
    samples, fields = sample_rows.shape
    lanes = 256
    per = lanes // fields
    chunks = samples // per
    targets = labels.reshape(chunks, per)

    chunk = (2, own, width)
    plane_buf = VMEM((pair, size, span, width), BF)
    vmem = pl.BlockSpec(memory_space=VMEM)
    update, score = pl.pallas_call(
        functools.partial(whole_kernel, size, length),
        out_shape=(
            jax.ShapeDtypeStruct(anchors.shape, F32),
            jax.ShapeDtypeStruct(targets.shape, F32),
        ),
        in_specs=[pl.BlockSpec(memory_space=pltpu.SMEM)] + [vmem] * 6,
        out_specs=(vmem, vmem),
        scratch_shapes=[
            VMEM((pair,) + chunk, BF),
            VMEM((pair, own, width), BF),
            VMEM((8, 128), jnp.int32),
            VMEM((size, 8, 128), jnp.int32),
            VMEM((pair, length) + chunk, BF),
            VMEM((blocks, size * span), BF),
            VMEM((size * span, blocks), BF),
            VMEM((rows, size * pair * span), BF),
            VMEM((size * pair * span, rows), BF),
            VMEM((chunks, lanes), jnp.int32),
            VMEM((chunks, rows, lanes), BF),
            VMEM((chunks, rows, lanes), BF),
            VMEM((chunks, lanes), F32),
            VMEM((rows, width), BF),
            plane_buf,
            plane_buf,
            plane_buf,
            plane_buf,
            VMEM((blocks, width), F32),
            VMEM((pair, length) + chunk, BF),
            VMEM((pair, 14) + chunk, BF),
            VMEM((pair, 2, own, width), BF),
            VMEM((pair, 2) + chunk, BF),
            VMEM((pair,) + chunk, F32),
            VMEM((pair, 2, own, width), BF),
            VMEM((pair, size, own, width), BF),
            DMA((2, pair * size)),
            DMA((2, pair * size)),
            DMA((2, pair * 16)),
            DMA((2, pair * 16)),
            DMA((2, pair)),
        ],
        compiler_params=pltpu.CompilerParams(
            collective_id=0, has_side_effects=True, vmem_limit_bytes=40 << 20
        ),
    )(block_counts, anchors, coefs, block_cols, sample_rows, targets, pair_weights)
    return update, score.reshape(-1)


def solution(mesh):
    return jax.shard_map(
        per_device,
        mesh=mesh,
        in_specs=(
            P("dev", None),
            P(("group", "dev"), None, None),
            P(("group", "dev"), None),
            P(("group", "dev")),
            P(("group", "dev"), None),
            P(("group", "dev")),
            P(),
        ),
        out_specs=(P("dev", None), P(("group", "dev"))),
        check_vma=False,
    )
```

```python
import functools

import jax
import jax.numpy as jnp
from jax import lax
from jax.experimental import pallas as pl
from jax.experimental.pallas import tpu as pltpu
from jax.sharding import PartitionSpec as P

BF = jnp.bfloat16
F32 = jnp.float32
MESH = pl.DeviceIdType.MESH
VMEM = pltpu.VMEM
DMA = pltpu.SemaphoreType.DMA
UNROLL = 8
NEAR = (1, -1, 2, -2)
FAR = 5
STEPS = 2
PART = 8


def dot(a, b, dims=((1,), (0,))):
    return lax.dot_general(a, b, (dims, ((), ())), preferred_element_type=F32)


def split(x):
    high = x.astype(BF)
    return high, (x - high.astype(F32)).astype(BF)


def whole_kernel(
    size,
    length,
    counts_ref,
    anchors_ref,
    coefs_ref,
    cols_ref,
    rows_ref,
    labels_ref,
    pairs_ref,
    update_ref,
    score_ref,
    mine,
    pair_out,
    ids_out,
    all_ids,
    every,
    placer,
    picker,
    weights,
    weights_t,
    rows_buf,
    ot_buf,
    pt_buf,
    z_buf,
    table_buf,
    fore_out,
    fore_in,
    back_out,
    back_in,
    acc_buf,
    sums,
    reduce_in,
    half_in,
    collect_out,
    total_buf,
    last_out,
    last_in,
    fore_sems,
    back_sems,
    gather_sems,
    reduce_sems,
    pair_sems,
):
    group, dev = lax.axis_index("group"), lax.axis_index("dev")
    core, z = dev % 2, dev // 2
    me = group * 2 + core
    parts = size // PART
    pair, _, own, width = mine.shape
    span = fore_out.shape[2]
    blocks = placer.shape[0]
    rows = table_buf.shape[0]
    rblocks, blk, deep = coefs_ref.shape
    slots = deep // blk
    chunks, lanes = rows_buf.shape
    per = labels_ref.shape[1]
    fields = lanes // per

    def iota(shape, dim):
        return lax.broadcasted_iota(jnp.int32, shape, dim)

    def hot(mask):
        return jnp.where(mask, 1.0, 0.0).astype(BF)

    my_part, my_place = me // PART, me % PART
    plane_base = z * 2

    def part_of(q):
        return lax.rem(my_part + (q + parts), parts)

    def plane_device(partner):
        return {"group": lax.div(partner, 2), "dev": plane_base + lax.rem(partner, 2)}

    def each_partner(q, act):
        base = part_of(q) * PART

        def one(j, carry):
            act(q * PART + j, base + lax.rem(my_place + j, PART))
            return carry

        lax.fori_loop(1 if q == 0 else 0, PART, one, 0)

    def plane_each(q, act, i, source, target, sems):
        def one(n, partner):
            act(
                pltpu.make_async_remote_copy(
                    src_ref=source(partner),
                    dst_ref=target.at[me],
                    send_sem=sems.at[0, i * size + n],
                    recv_sem=sems.at[1, i * size + n],
                    device_id=plane_device(partner),
                    device_id_type=MESH,
                )
            )

        each_partner(q, one)

    def start(copy):
        copy.start()

    def wait_recv(copy):
        copy.wait_recv()

    def wait_send(copy):
        copy.wait_send()

    def ring_device(s):
        return {"dev": (dev + 2 * s + 2 * length) % (2 * length)}

    def ring_copy(n, i, s, source, target, sems):
        return pltpu.make_async_remote_copy(
            src_ref=source,
            dst_ref=target,
            send_sem=sems.at[0, i * 16 + n],
            recv_sem=sems.at[1, i * 16 + n],
            device_id=ring_device(s),
            device_id_type=MESH,
        )

    def near(k):
        return (z + k + 2 * length) % length

    barrier = pltpu.get_barrier_semaphore()

    def greet(n, partner):
        pl.semaphore_signal(barrier, inc=1, device_id=plane_device(partner), device_id_type=MESH)

    ring_mates = NEAR + (3, -3, FAR, -FAR)
    for s in ring_mates:
        pl.semaphore_signal(barrier, inc=1, device_id=ring_device(s), device_id_type=MESH)
    for q in range(parts):
        each_partner(q, greet)

    anchors = anchors_ref[...]
    held = anchors.shape[0]
    row = iota((pair * own, held), 0)
    col = iota((pair * own, held), 1)

    def pick(place):
        wanted = (row % own) * blk + place * pair + row // own
        return dot(hot(col == wanted), anchors).astype(BF).reshape(pair_out.shape)

    pair_out[...] = pick(me + 1 - 2 * core)
    kept = pick(me)
    for i in range(pair):
        mine[i, core] = kept[i]
    line = jnp.concatenate([cols_ref[b : b + 1, :] for b in range(rblocks)] * (128 // span), axis=1)
    ids_out[...] = jnp.broadcast_to(line, ids_out.shape)
    pl.semaphore_wait(barrier, size - 1 + len(ring_mates))

    pair_copies = [
        pltpu.make_async_remote_copy(
            src_ref=pair_out.at[i],
            dst_ref=mine.at[i, core],
            send_sem=pair_sems.at[0, i],
            recv_sem=pair_sems.at[1, i],
            device_id={"dev": dev + 1 - 2 * core},
            device_id_type=MESH,
        )
        for i in range(pair)
    ]
    for copy in pair_copies:
        copy.start()
    own_ids = lambda partner: ids_out
    for q in range(parts):
        plane_each(q, start, 0, own_ids, all_ids, back_sems)
    all_ids[me] = ids_out[...]

    def gather_own(i, first=0, last=6):
        ways = tuple(enumerate((FAR, -FAR) + NEAR))[first:last]
        return [ring_copy(n, i, s, mine.at[i], every.at[i, z], gather_sems) for n, s in ways]

    def gather_on(i, h):
        held_at = near(-FAR if h == 0 else FAR)
        piece = every.at[i, held_at]
        copies = [ring_copy(6 + 5 * h + n, i, s, piece, piece, gather_sems) for n, s in enumerate(NEAR)]
        half = every.at[i, held_at, h]
        copies.append(ring_copy(10 + 5 * h, i, 3 if h == 0 else -3, half, half, gather_sems))
        return copies

    def gather_start(i):
        for copy in gather_own(i) if i == 0 else gather_own(i, 0, 2):
            copy.start()
        every[i, z] = mine[i]

    def gather_forward(i):
        if i:
            for copy in gather_own(i, 2):
                copy.start()
        for h in (0, 1):
            gather_own(i, h, h + 1)[0].wait_recv()
            for copy in gather_on(i, h):
                copy.start()

    def gather_end(i):
        for copy in gather_own(i, 2) + gather_on(i, 0) + gather_on(i, 1):
            copy.wait_recv()

    def gather_sent():
        for i in range(pair):
            for copy in gather_own(i) + gather_on(i, 0) + gather_on(i, 1):
                copy.wait_send()

    for i in range(pair):
        pair_copies[i].wait()
        gather_start(i)

    member = hot(iota((lanes, per), 0) // fields == iota((lanes, per), 1))
    total_buf[...] = jnp.zeros(total_buf.shape, F32)
    off = jnp.where(iota((fields, fields), 0) == iota((fields, fields), 1), 0.0, pairs_ref[...])
    sym = (off + off.T).astype(BF)
    repeat = hot(iota((lanes, fields), 0) % fields == iota((lanes, fields), 1))
    mix = dot(dot(repeat, sym).astype(BF), repeat, ((1,), (1,)))
    mix = jnp.where(iota((lanes, lanes), 0) // fields == iota((lanes, lanes), 1) // fields, mix, 0.0)
    mix = mix.astype(BF)
    rows_buf[...] = jnp.concatenate(
        [rows_ref[pl.ds(u, chunks, stride=per), :] for u in range(per)], axis=1
    )
    row_iota = iota((rows, lanes), 0)

    def prepare(step, carry):
        for u in range(UNROLL):
            c = step * UNROLL + u
            ot = hot(row_iota == rows_buf[pl.ds(c, 1), :])
            ot_buf[c] = ot
            pt_buf[c] = dot(ot, mix).astype(BF)
        return carry

    lax.fori_loop(0, chunks // UNROLL, prepare, 0)
    for i in range(pair):
        gather_forward(i)

    for q in range(parts):
        plane_each(q, wait_recv, 0, own_ids, all_ids, back_sems)
        plane_each(q, wait_send, 0, own_ids, all_ids, back_sems)
    quarter = iota((1, 128), 1) // span
    block_iota = iota((blocks, 128), 0)
    together = 128 // span
    for t in range(size // together):
        line = all_ids[t * together, 0:1, :]
        for u in range(1, together):
            line = jnp.where(quarter == u, all_ids[t * together + u, 0:1, :], line)
        found = jnp.where(block_iota == line, 1.0, 0.0)
        placer[:, t * 128 : (t + 1) * 128] = found.astype(BF)
        picker[t * 128 : (t + 1) * 128, :] = found.T.astype(BF)

    flat = coefs_ref[...].reshape(rows, deep)
    tile = 256
    for t in range(weights.shape[1] // tile):
        n = iota((1, tile), 1) + t * tile
        slot, block = n % slots, (n // slots) % rblocks
        offset = (n // span) % size * pair + n // (span * size)
        order = hot(iota((deep, tile), 0) == slot * blk + offset)
        bound = jnp.where(block == 0, counts_ref[0], counts_ref[1])
        block = jnp.where(slot < bound, block, rblocks)
        value = jnp.where(iota((rows, tile), 0) // blk == block, dot(flat, order), 0.0)
        weights[:, t * tile : (t + 1) * tile] = value.astype(BF)
        weights_t[t * tile : (t + 1) * tile, :] = value.T.astype(BF)

    depth = PART * span

    def from_part(base, part):
        return pl.ds(pl.multiple_of(base + part * depth, depth), depth)

    def fore(act, i, q):
        plane_each(q, act, i, lambda partner: fore_out.at[i, partner], fore_in.at[i], fore_sems)

    def back(act, i, q):
        plane_each(q, act, i, lambda partner: back_out.at[i, partner], back_in.at[i], back_sems)

    def final(act, i):
        for q in range(parts):
            plane_each(
                q, act, i, lambda partner: last_out.at[i, lax.rem(partner, 2)], last_in.at[i], fore_sems
            )

    def forward():
        for i in range(pair):
            gather_end(i)
            for q in range(parts):
                part = part_of(q)
                picks = picker[from_part(0, part), :]
                picked = dot(picks, every[i].reshape(blocks, width)).astype(BF)
                fore_out[i, pl.ds(part * PART, PART)] = picked.reshape(PART, span, width)
                fore(start, i, q)
            fore_in[i, me] = fore_out[i, me]
        gather_sent()
        table = jnp.zeros((rows, width), F32)
        for i in range(pair):
            for q in range(parts):
                fore(wait_recv, i, q)
                part = part_of(-q)
                got = fore_in[i, pl.ds(part * PART, PART)].reshape(depth, width)
                table = table + dot(weights[:, from_part(i * size * span, part)], got)
        table_buf[...] = table.astype(BF)

    def interact():
        table = table_buf[...]
        gram = dot(table, table, ((1,), (1,))).astype(BF)

        def first(step, carry):
            for u in range(UNROLL):
                c = step * UNROLL + u
                q = dot(gram, ot_buf[c]) * pt_buf[c].astype(F32)
                z_buf[pl.ds(c, 1), :] = jnp.sum(q, axis=0, keepdims=True)
            return carry

        lax.fori_loop(0, chunks // UNROLL, first, 0)
        high, low = split(z_buf[...])
        score = 0.5 * (dot(high, member) + dot(low, member))
        score_ref[...] = score
        slope = 1.0 / (1.0 + jnp.exp(-score)) - labels_ref[...].astype(F32)
        z_buf[...] = dot(slope.astype(BF), member, ((1,), (1,)))

        def second(step, total):
            for u in range(UNROLL):
                c = step * UNROLL + u
                w = z_buf[pl.ds(c, 1), :].astype(BF) * pt_buf[c]
                total = total + dot(w, ot_buf[c], ((1,), (1,)))
            return total

        total = lax.fori_loop(0, chunks // UNROLL, second, jnp.zeros((rows, rows), F32))
        high, low = split(total)
        return (dot(high, table) + dot(low, table)).astype(BF)

    def first_stage(i):
        copies = []
        for a, s in enumerate(NEAR):
            for h, far in ((0, -FAR), (1, FAR)):
                source, target = sums.at[i, near(s + far)], reduce_in.at[i, 4 * h + a]
                copies.append(ring_copy(4 * h + a, i, s, source, target, reduce_sems))
        for h, s in ((0, -3), (1, 3)):
            copies.append(ring_copy(8 + h, i, s, sums.at[i, near(8), h], half_in.at[i, h], reduce_sems))
        return copies

    def direct_stage(i):
        return [
            ring_copy(10 + a, i, s, sums.at[i, near(s)], reduce_in.at[i, 8 + a], reduce_sems)
            for a, s in enumerate(NEAR)
        ]

    def far_stage(i):
        return [
            ring_copy(14 + h, i, s, collect_out.at[i, h], reduce_in.at[i, 12 + h], reduce_sems)
            for h, s in ((0, -FAR), (1, FAR))
        ]

    def backward(row_grad):
        for i in range(pair):
            for q in range(parts):
                part = part_of(q)
                value = dot(weights_t[from_part(i * size * span, part), :], row_grad).astype(BF)
                back_out[i, pl.ds(part * PART, PART)] = value.reshape(PART, span, width)
                if i:
                    back(wait_send, i - 1, q)
                back(start, i, q)
            back_in[i, me] = back_out[i, me]
        for i in range(pair):
            for q in range(parts):
                fore(wait_send, i, q)
        for i in range(pair):
            for q in range(parts):
                back(wait_recv, i, q)
                part = part_of(-q)
                got = back_in[i, pl.ds(part * PART, PART)].reshape(depth, width)
                value = dot(placer[:, from_part(0, part)], got)
                if q:
                    value = value + acc_buf[...]
                if q < parts - 1:
                    acc_buf[...] = value
                else:
                    sums[i] = value.astype(BF).reshape(length, 2, own, width)
            for copy in first_stage(i) + (direct_stage(i) if i < pair - 1 else []):
                copy.start()

    def collect(i):
        far = far_stage(i)
        for copy in first_stage(i):
            copy.wait_recv()
        for h, s in ((0, -FAR), (1, FAR)):
            value = sums[i, near(s)].astype(F32)
            for a in range(4):
                value = value + reduce_in[i, 4 * h + a].astype(F32)
            collect_out[i, h, 1 - h] = value[1 - h].astype(BF)
            collect_out[i, h, h] = (value[h] + half_in[i, h].astype(F32)).astype(BF)
            far[h].start()

    def reduced(i):
        grad = sums[i, z].astype(F32)
        for copy in direct_stage(i) + far_stage(i):
            copy.wait_recv()
        for a in range(6):
            grad = grad + reduce_in[i, 8 + a].astype(F32)
        return grad

    def one_step(step, carry):
        @pl.when(step > 0)
        def _():
            for i in range(pair):
                gather_forward(i)

        forward()
        backward(interact())
        for i in range(pair):
            collect(i)
            if i == 0:
                for copy in direct_stage(pair - 1):
                    copy.start()
        for i in range(pair):
            grad = reduced(i)
            total = total_buf[i] + grad
            total_buf[i] = total
            mine[i] = (mine[i].astype(F32) - grad).astype(BF)

            @pl.when(step < STEPS - 1)
            def _():
                gather_start(i)

            @pl.when(step == STEPS - 1)
            def _():
                last_out[i] = (-total).astype(BF)
                final(start, i)
                last_in[i, me] = last_out[i, core]

        for i in range(pair):
            for copy in first_stage(i) + direct_stage(i) + far_stage(i):
                copy.wait_send()
        for q in range(parts):
            back(wait_send, pair - 1, q)
        return carry

    lax.fori_loop(0, STEPS, one_step, 0)

    source = iota((1, held), 1)
    place = (source % own) * blk + (source // own) % size * pair + source // (own * size)
    order = hot(iota((held, held), 0) == place)
    for i in range(pair):
        final(wait_recv, i)
    update_ref[...] = dot(order, last_in[...].reshape(held, width))
    for i in range(pair):
        final(wait_send, i)


def per_device(anchors, coefs, block_cols, block_counts, sample_rows, labels, pair_weights):
    length = lax.axis_size("dev") // 2
    size = lax.axis_size("group") * 2
    rblocks, slots = block_cols.shape
    blk = coefs.shape[1]
    width = anchors.shape[1]
    own = anchors.shape[0] // blk
    span = rblocks * slots
    blocks = length * 2 * own
    pair = blk // size
    rows = rblocks * blk
    samples, fields = sample_rows.shape
    lanes = 256
    per = lanes // fields
    chunks = samples // per
    targets = labels.reshape(chunks, per)

    chunk = (2, own, width)
    plane_buf = VMEM((pair, size, span, width), BF)
    vmem = pl.BlockSpec(memory_space=VMEM)
    update, score = pl.pallas_call(
        functools.partial(whole_kernel, size, length),
        out_shape=(
            jax.ShapeDtypeStruct(anchors.shape, F32),
            jax.ShapeDtypeStruct(targets.shape, F32),
        ),
        in_specs=[pl.BlockSpec(memory_space=pltpu.SMEM)] + [vmem] * 6,
        out_specs=(vmem, vmem),
        scratch_shapes=[
            VMEM((pair,) + chunk, BF),
            VMEM((pair, own, width), BF),
            VMEM((8, 128), jnp.int32),
            VMEM((size, 8, 128), jnp.int32),
            VMEM((pair, length) + chunk, BF),
            VMEM((blocks, size * span), BF),
            VMEM((size * span, blocks), BF),
            VMEM((rows, size * pair * span), BF),
            VMEM((size * pair * span, rows), BF),
            VMEM((chunks, lanes), jnp.int32),
            VMEM((chunks, rows, lanes), BF),
            VMEM((chunks, rows, lanes), BF),
            VMEM((chunks, lanes), F32),
            VMEM((rows, width), BF),
            plane_buf,
            plane_buf,
            plane_buf,
            plane_buf,
            VMEM((blocks, width), F32),
            VMEM((pair, length) + chunk, BF),
            VMEM((pair, 14) + chunk, BF),
            VMEM((pair, 2, own, width), BF),
            VMEM((pair, 2) + chunk, BF),
            VMEM((pair,) + chunk, F32),
            VMEM((pair, 2, own, width), BF),
            VMEM((pair, size, own, width), BF),
            DMA((2, pair * size)),
            DMA((2, pair * size)),
            DMA((2, pair * 16)),
            DMA((2, pair * 16)),
            DMA((2, pair)),
        ],
        compiler_params=pltpu.CompilerParams(
            collective_id=0, has_side_effects=True, vmem_limit_bytes=40 << 20
        ),
    )(block_counts, anchors, coefs, block_cols, sample_rows, targets, pair_weights)
    return update, score.reshape(-1)


def solution(mesh):
    return jax.shard_map(
        per_device,
        mesh=mesh,
        in_specs=(
            P("dev", None),
            P(("group", "dev"), None, None),
            P(("group", "dev"), None),
            P(("group", "dev")),
            P(("group", "dev"), None),
            P(("group", "dev")),
            P(),
        ),
        out_specs=(P("dev", None), P(("group", "dev"))),
        check_vma=False,
    )
```
